32 devices in a mesh: parts: 2 (over y), slab: 8 (over z, x), sub: 2 (over core).
Axes of the slice: x: 2, y: 2, z: 4, core: 2. Of those that a mesh axis runs over, the one named last changes fastest.
Arguments:
- node_feat: bfloat16 [16384, 512], P(('parts', 'slab', 'sub')), parts along dimension 0, may hold values from -6 to 6
- self_weight: bfloat16 [512, 512], replicated, may hold values from -0.25 to 0.25
- neigh_weight: bfloat16 [512, 512], replicated, may hold values from -0.25 to 0.25
- block_tiles: bfloat16 [128, 3, 6, 128, 128], P(('parts', 'slab', 'sub')), parts along dimension 0, may hold values from -6 to 6
- source_block: int32 [128, 3, 6], P(('parts', 'slab', 'sub')), parts along dimension 0, may hold values from 0 to 7
- edge_counts: int32 [128, 3, 6], P(('parts', 'slab', 'sub')), parts along dimension 0, may hold values from 0 to 128
- normalizer: int32 [16384], P(('parts', 'slab', 'sub')), parts along dimension 0, may hold values from 16 to 64
- cotangent: bfloat16 [16384, 512], P(('parts', 'slab', 'sub')), parts along dimension 0, may hold values from -6 to 6
Outputs:
- node_out: bfloat16 [16384, 512], P(('parts', 'slab', 'sub')), parts along dimension 0
- node_grad: bfloat16 [16384, 512], P(('parts', 'slab', 'sub')), parts along dimension 0
The draws below stay inside these ranges and needn't reach their ends.
There are 2 independent parts, one for each index of `parts`. The reference program is written for one: setup_inputs(seed, part) draws one part's arguments, and reference() takes and returns one part's arrays. A program takes and returns all parts, laid end to end along the dimension named above; an argument that names none is the same for every part. Nothing has to cross between parts.
Inputs may be any that keep to these rules, and one draw needn't show every extreme that they name: `edge_counts`: A slot with edge count 0 adds nothing.
All inputs are finite; a program needn't handle non-finite values.
Results may differ from the reference program's by a relative error of at most 0.01.
Values may be sent and summed in bfloat16 or wider, within the bound.
No kernel may reach another device: no remote copies, remote signals or barrier semaphores. Data moves between devices by JAX's collectives and lax.ppermute only.
A program may use at most 64 MiB of HBM per device.

```python
import jax
import jax.numpy as jnp
from jax import lax

FEAT = 512
HIDDEN_SIZE = 512
BLOCK = 128
SLOTS = 6
ROWS_DEV = 512
SLAB = 1024
NODES = 8192
NBLK = 64
SBLK = 8
N_SLAB = 8
N_SUB = 2


def place_ends(array, own_key, least, largest):
    longest = array.shape.index(max(array.shape))
    spots = []
    for shift in (0, 1):
        where = [jax.random.randint(jax.random.fold_in(own_key, axis), (), 0, length) for axis, length in enumerate(array.shape)]
        where[longest] = (where[longest] + shift) % array.shape[longest]
        spots.append(tuple(where))
    return array.at[spots[0]].set(least).at[spots[1]].set(largest)


def level_of(stream_key, extent, shards, least, largest):
    def one(dim, blocks):
        steps = jax.random.uniform(jax.random.fold_in(jax.random.fold_in(stream_key, 6), dim), (blocks,), jnp.float32, least / len(shards), largest / len(shards))
        return jnp.repeat(jnp.exp(steps), extent[dim] // blocks).reshape((-1,) + (1,) * (len(extent) - dim - 1))

    loudness = one(*shards[0])
    for cut in shards[1:]:
        loudness = loudness * one(*cut)
    return loudness


def scatter_about(rng, shape, width, most, pieces=(), held_as=jnp.bfloat16):
    result = width * jax.random.normal(rng, shape, jnp.float32)
    if pieces:
        result = result * level_of(rng, shape, pieces, -0.22, 0.18)
    return jnp.clip(result, -most, most).astype(held_as)


def setup_inputs(seed: int = 0, part: int = 0) -> dict:
    streams_of = jax.random.split(jax.random.key(seed), 9)
    part_splits = jax.random.split(jax.random.fold_in(streams_of[8], part), 9)
    return {
        "node_feat": scatter_about(part_splits[0], (NODES, FEAT), 1.0, 6.0, ((0, 16),)),
        "self_weight": scatter_about(streams_of[1], (FEAT, HIDDEN_SIZE), FEAT ** -0.5, 0.25),
        "neigh_weight": scatter_about(streams_of[2], (FEAT, HIDDEN_SIZE), FEAT ** -0.5, 0.25),
        "block_tiles": scatter_about(part_splits[3], (NBLK, 3, SLOTS, BLOCK, BLOCK), 1.0, 6.0, ((0, 16),)),
        "source_block": place_ends(jax.random.randint(part_splits[4], (NBLK, 3, SLOTS), 0, SBLK), jax.random.fold_in(part_splits[4], 1), 0, SBLK - 1).astype(jnp.int32),
        "edge_counts": place_ends(jax.random.randint(part_splits[5], (NBLK, 3, SLOTS), 0, BLOCK + 1), jax.random.fold_in(part_splits[5], 1), 0, BLOCK).astype(jnp.int32),
        "normalizer": place_ends(jax.random.randint(part_splits[6], (NODES,), 16, 65), jax.random.fold_in(part_splits[6], 1), 16, 64).astype(jnp.int32),
        "cotangent": scatter_about(part_splits[7], (NODES, HIDDEN_SIZE), 1.0, 6.0, ((0, 16),)),
    }


def weighted_tiles(block_tiles, edge_counts):
    scale = edge_counts.astype(jnp.float32) / BLOCK
    return (block_tiles.astype(jnp.float32) * scale[..., None, None]).astype(jnp.bfloat16)

def silu_grad(pre_act):
    logistic = jax.nn.sigmoid(pre_act)
    return logistic * (1.0 + pre_act * (1.0 - logistic))

def reference(node_feat, self_weight, neigh_weight, block_tiles, source_block, edge_counts, normalizer, cotangent):
    slab_blocks = SLAB // BLOCK
    dest_blocks = ROWS_DEV // BLOCK
    weighted = weighted_tiles(block_tiles, edge_counts).reshape(N_SLAB, slab_blocks, 3, SLOTS, BLOCK, BLOCK)
    sources = source_block.reshape(N_SLAB, slab_blocks, 3, SLOTS)
    slabs = node_feat.reshape(N_SLAB, slab_blocks, BLOCK, FEAT)
    slab_ids = jnp.arange(N_SLAB, dtype=jnp.int32)

    def forward_slab(inputs):
        slab_id, slab_tiles, slab_sources = inputs
        summed = jnp.zeros((slab_blocks, BLOCK, FEAT), jnp.float32)
        for offset in range(3):
            other = ((slab_id + offset - 1) % N_SLAB).astype(jnp.int32)
            source_rows = lax.dynamic_index_in_dim(slabs, other, 0, keepdims=False)
            picked = source_rows[slab_sources[:, offset]]
            summed = summed + jnp.einsum('bkij,bkjf->bif', slab_tiles[:, offset].astype(jnp.float32), picked.astype(jnp.float32))
        return summed
    messages = lax.map(forward_slab, (slab_ids, weighted, sources)).reshape(NODES, FEAT)
    scale_rows = normalizer.astype(jnp.float32)[:, None]
    aggregate = (messages / scale_rows).astype(jnp.bfloat16)
    pre_act = jnp.dot(node_feat, self_weight, preferred_element_type=jnp.float32) + jnp.dot(aggregate, neigh_weight, preferred_element_type=jnp.float32)
    node_out = jax.nn.silu(pre_act).astype(jnp.bfloat16)
    pre_grad = (cotangent.astype(jnp.float32) * silu_grad(pre_act)).astype(jnp.bfloat16)
    agg_grad = (jnp.dot(pre_grad, neigh_weight.T, preferred_element_type=jnp.float32) / scale_rows).astype(jnp.bfloat16)
    grad_blocks = agg_grad.reshape(N_SLAB, slab_blocks, BLOCK, FEAT)
    block_ids = jnp.arange(slab_blocks, dtype=jnp.int32)

    def backward_slab(inputs):
        slab_tiles, slab_sources, slab_grad = inputs
        results = []
        for offset in range(3):
            spread = jnp.einsum('bkij,bif->bkjf', slab_tiles[:, offset].astype(jnp.float32), slab_grad.astype(jnp.float32))
            selector = (slab_sources[:, offset][..., None] == block_ids).astype(jnp.float32)
            spread = spread.reshape(N_SUB, dest_blocks, SLOTS, BLOCK, FEAT)
            selector = selector.reshape(N_SUB, dest_blocks, SLOTS, slab_blocks)
            placed = jnp.einsum('udkq,udkjf->uqjf', selector, spread)
            results.append(placed.astype(jnp.bfloat16))
        return jnp.stack(results)
    partials = lax.map(backward_slab, (weighted, sources, grad_blocks))
    returned = jnp.zeros((N_SLAB, slab_blocks, BLOCK, FEAT), jnp.float32)
    for offset in range(3):
        landed = lax.optimization_barrier(jnp.sum(partials[:, offset].astype(jnp.float32), axis=1))
        returned = returned + jnp.roll(landed, offset - 1, axis=0)
    node_grad = (jnp.dot(pre_grad, self_weight.T, preferred_element_type=jnp.float32) + returned.reshape(NODES, FEAT)).astype(jnp.bfloat16)
    return (node_out, node_grad)
```

```python
import jax
import jax.numpy as jnp
from jax import lax
from jax.experimental import pallas as pl
from jax.experimental.pallas import tpu as pltpu
from jax.sharding import PartitionSpec as P

ROWS = ("parts", "slab", "sub")


def dense_kernel(info, sources, counts, tiles, fwd, mine, other, total):
    i = pl.program_id(0)
    j, u = info[0], info[1]
    slots, size = tiles.shape[2], tiles.shape[3]
    blocks = total.shape[0]
    half = blocks // 2
    total[...] = jnp.zeros_like(total)
    for k in range(slots):
        at = (i * 3 + j) * slots + k
        b = sources[at]
        place = jnp.bitwise_xor(b // half, u) * half + b % half
        scale = counts[at].astype(jnp.float32) * (1.0 / size)
        total[place] += tiles[0, 0, k].astype(jnp.float32) * scale
    for b in range(blocks):
        block = total[b]
        fwd[:, b * size:(b + 1) * size] = block.astype(fwd.dtype)
        turned = block.T.astype(fwd.dtype)
        if b < half:
            mine[b * size:(b + 1) * size, :] = turned
        else:
            other[(b - half) * size:(b - half + 1) * size, :] = turned


def dense(info, sources, counts, tiles):
    local, _, slots, size, _ = tiles.shape
    rows = local * size
    kind = tiles.dtype
    return pl.pallas_call(
        dense_kernel,
        grid_spec=pltpu.PrefetchScalarGridSpec(
            num_scalar_prefetch=3,
            grid=(local,),
            in_specs=[
                pl.BlockSpec((1, 1, slots, size, size), lambda i, n, s, c: (i, n[0], 0, 0, 0)),
            ],
            out_specs=[
                pl.BlockSpec((size, 2 * rows), lambda i, n, s, c: (i, 0)),
                pl.BlockSpec((rows, size), lambda i, n, s, c: (0, i)),
                pl.BlockSpec((rows, size), lambda i, n, s, c: (0, i)),
            ],
            scratch_shapes=[pltpu.VMEM((2 * local, size, size), jnp.float32)],
        ),
        out_shape=[
            jax.ShapeDtypeStruct((rows, 2 * rows), kind),
            jax.ShapeDtypeStruct((rows, rows), kind),
            jax.ShapeDtypeStruct((rows, rows), kind),
        ],
        compiler_params=pltpu.CompilerParams(vmem_limit_bytes=16 << 20),
        cost_estimate=pl.CostEstimate(
            flops=4 * local * slots * size * size,
            bytes_accessed=2 * local * (slots + 4 * local) * size * size,
            transcendentals=0,
        ),
    )(info, sources, counts, tiles)


def mm(a, b):
    return jnp.dot(a, b, preferred_element_type=jnp.float32)


def mmt(a, b):
    return lax.dot_general(a, b, (((1,), (1,)), ((), ())), preferred_element_type=jnp.float32)


def after(value, *earlier):
    return lax.optimization_barrier((value, *earlier))[0]


def per_device(x, w_self, w_neigh, tiles, source_block, edge_counts, normalizer, cotangent):
    n_slab = lax.axis_size("slab")
    ring = range(n_slab)
    pair = [(i, i ^ 1) for i in ring]
    diag = [(i, (i + (1 if i % 2 else -1)) % n_slab) for i in ring]
    hop = [(i, (i + (-2 if i % 2 else 2)) % n_slab) for i in ring]
    back = [(b, a) for a, b in hop]
    swap = [(0, 1), (1, 0)]

    def slab(v, route):
        return lax.ppermute(v, "slab", route)

    def sub(v):
        return lax.ppermute(v, "sub", swap)

    rows, width = x.shape
    cut = rows // 2
    odd = lax.axis_index("slab") % 2
    u = lax.axis_index("sub")
    kind = x.dtype
    sources = source_block.reshape(-1)
    counts = edge_counts.reshape(-1)

    def build(j):
        return dense(jnp.stack([j, u]).astype(jnp.int32), sources, counts, tiles)

    xa = slab(x[:cut], pair)
    x_sib = sub(x)
    fx, mx, ox = build(2 - 2 * odd)
    xb = slab(after(x[cut:], fx), pair)
    zb = slab(after(x[cut:], fx), diag)
    za = slab(xa, hop)
    fz, mz, oz = build(2 * odd)
    fo, mo, oo = build(jnp.ones_like(odd))
    mx2, mz2, mo2 = sub(ox), sub(oz), sub(oo)
    xa_sib, za_sib, xb_sib, zb_sib = sub(xa), sub(za), sub(xb), sub(zb)
    own = mm(x, w_self)
    messages = mm(fo[:, :rows], x) + mm(fo[:, rows:], x_sib)
    c0, c1, c2, c3, c4 = (k * cut for k in range(5))
    messages += mm(fx[:, c0:c1], xa) + mm(fx[:, c2:c3], xa_sib)
    messages += mm(fz[:, c0:c1], za) + mm(fz[:, c2:c3], za_sib)
    messages += mm(fx[:, c1:c2], xb) + mm(fz[:, c1:c2], zb)
    messages += mm(fx[:, c3:c4], xb_sib) + mm(fz[:, c3:c4], zb_sib)

    norm = normalizer.astype(jnp.float32)[:, None]
    aggregate = (messages / norm).astype(kind)
    pre = own + mm(aggregate, w_neigh)
    q = jax.nn.sigmoid(pre)
    node_out = (pre * q).astype(kind)
    pre_grad = (cotangent.astype(jnp.float32) * (q * (1.0 + pre * (1.0 - q)))).astype(kind)
    g = (mmt(pre_grad, w_neigh) / norm).astype(kind)
    g_sib = sub(g)

    pz = (mm(mz, g) + mm(mz2, g_sib)).astype(kind)
    ra = slab(pz[:cut], back)
    px = mm(mx, g) + mm(mx2, g_sib)
    rzb = slab(pz[cut:], diag)
    rxb = slab(px[cut:].astype(kind), pair)
    own_grad = mmt(pre_grad, w_self) + mm(mo, g) + mm(mo2, g_sib)
    rxa = slab((px[:cut] + ra.astype(jnp.float32)).astype(kind), pair)
    low = own_grad[:cut] + rxa.astype(jnp.float32)
    high = own_grad[cut:] + rxb.astype(jnp.float32) + rzb.astype(jnp.float32)
    node_grad = jnp.concatenate([low, high], axis=0).astype(kind)
    return (node_out, node_grad)


def solution(mesh):
    whole = P(None, None)
    return jax.shard_map(
        per_device,
        mesh=mesh,
        in_specs=(
            P(ROWS, None),
            whole,
            whole,
            P(ROWS, None, None, None, None),
            P(ROWS, None, None),
            P(ROWS, None, None),
            P(ROWS),
            P(ROWS, None),
        ),
        out_specs=(P(ROWS, None), P(ROWS, None)),
        check_vma=False,
    )
```

```python
import functools

import jax
import jax.numpy as jnp
from jax import lax
from jax.experimental import pallas as pl
from jax.experimental.pallas import tpu as pltpu
from jax.sharding import PartitionSpec as P

ROWS = ("parts", "slab", "sub")
VMEM = pl.BlockSpec(memory_space=pltpu.VMEM)
SMEM = pl.BlockSpec(memory_space=pltpu.SMEM)
ANY = pl.BlockSpec(memory_space=pl.ANY)


def dot(a, b):
    return jnp.dot(a, b, preferred_element_type=jnp.float32)


def dot_t(a, b):
    return lax.dot_general(a, b, (((1,), (1,)), ((), ())), preferred_element_type=jnp.float32)


def call(kernel, outs, *args, specs=None, out_specs=None, scratch=(), flops=1 << 26, name=None):
    single = not isinstance(outs, list)
    return pl.pallas_call(
        kernel,
        in_specs=specs or [VMEM] * len(args),
        out_specs=out_specs or (VMEM if single else [VMEM] * len(outs)),
        out_shape=outs,
        scratch_shapes=scratch,
        compiler_params=pltpu.CompilerParams(vmem_limit_bytes=12 << 20),
        cost_estimate=pl.CostEstimate(flops=1 << 36, bytes_accessed=1 << 30, transcendentals=0),
        name=name,
    )(*args)


OFFSET = {
    "own": lambda odd: 1,
    "pair": lambda odd: 2 - 2 * odd,
    "across": lambda odd: 2 * odd,
}


def dense_kernel(roles, known, info, sources, counts, tiles, *refs):
    count = len(roles)
    fwds, refs = refs[:known], refs[known:]
    outs, refs = refs[:count], refs[count:]
    last = len(refs) > 3
    if last:
        mine, send, buffer, total, in_sem, turned, out_sem = refs
    else:
        buffer, total, in_sem = refs
    local, slots, size = buffer.shape[1], buffer.shape[2], buffer.shape[3]
    rows = local * size
    u = info[1]
    offsets = [OFFSET[role](info[0]) for role in roles]

    def load(r, i):
        return pltpu.make_async_copy(tiles.at[i, offsets[r]], buffer.at[r, i], in_sem.at[r, i])

    def place_of(b):
        at = (b % local) * size
        return b // local, slice(at, at + size)

    stores = []

    def hand_out(n):
        for h, out in enumerate((mine, send)):
            part = pl.ds(n * rows, rows)
            store = pltpu.make_async_copy(turned.at[h, part], out.at[part], out_sem.at[h, n])
            store.start()
            stores.append(store)

    for r in range(count):
        for i in range(local):
            load(r, i).start()
    if last:
        for n, fwd in enumerate(fwds):
            for i in range(local):
                rows_i = slice(i * size, (i + 1) * size)
                for b in range(2 * local):
                    h, at = place_of(b)
                    block = fwd[rows_i, b * size:(b + 1) * size]
                    turned[h, n * rows + at.start:n * rows + at.stop, rows_i] = block.T
            hand_out(n)
    for r in range(count):
        n = known + r
        for i in range(local):
            load(r, i).wait()
            total[...] = jnp.zeros_like(total)
            for k in range(slots):
                b = sources[offsets[r], i, k]
                place = jnp.bitwise_xor(b // local, u) * local + b % local
                scale = counts[offsets[r], i, k].astype(jnp.float32) * (1.0 / size)
                total[place] += buffer[r, i, k].astype(jnp.float32) * scale
            rows_i = slice(i * size, (i + 1) * size)
            for b in range(2 * local):
                block = total[b].astype(outs[r].dtype)
                outs[r][rows_i, b * size:(b + 1) * size] = block
                if last:
                    h, at = place_of(b)
                    turned[h, n * rows + at.start:n * rows + at.stop, rows_i] = block.T
        if last:
            hand_out(n)
    for store in stores:
        store.wait()


def dense(roles, built, last, info, sources, counts, tiles):
    local, _, slots, size, _ = tiles.shape
    rows = local * size
    count, every = len(roles), len(roles) + len(built)
    kind = tiles.dtype
    hbm = pl.BlockSpec(memory_space=pltpu.HBM)
    outs = [jax.ShapeDtypeStruct((rows, 2 * rows), kind)] * count
    out_specs = [VMEM] * count
    scratch = [
        pltpu.VMEM((count, local, slots, size, size), kind),
        pltpu.VMEM((2 * local, size, size), jnp.float32),
        pltpu.SemaphoreType.DMA((count, local)),
    ]
    if last:
        outs += [pltpu.HBM((every * rows, rows), kind)] * 2
        out_specs += [hbm] * 2
        scratch += [
            pltpu.VMEM((2, every * rows, rows), kind),
            pltpu.SemaphoreType.DMA((2, every)),
        ]
    return call(
        functools.partial(dense_kernel, roles, len(built)),
        outs,
        info, sources, counts, tiles, *built,
        specs=[SMEM, SMEM, SMEM, hbm] + [VMEM] * len(built),
        out_specs=out_specs,
        scratch=scratch,
        flops=count << 28,
        name="dense_" + roles[0],
    )


def local_kernel(adj, x, x_sib, messages):
    rows = x.shape[0]
    messages[...] = dot(adj[:, :rows], x[...]) + dot(adj[:, rows:], x_sib[...])


def self_kernel(x, w_self, own):
    own[...] = dot(x[...], w_self[...])


def gather_kernel(starts, messages, *refs):
    count = len(starts)
    adjs, feats, out = refs[:count], refs[count:2 * count], refs[2 * count]
    total = messages[...]
    for start, adj, feat in zip(starts, adjs, feats):
        total += dot(adj[:, start:start + feat.shape[0]], feat[...])
    out[...] = total


def gather(messages, starts, adjs, feats):
    out = jax.ShapeDtypeStruct(messages.shape, jnp.float32)
    return call(functools.partial(gather_kernel, starts), out, messages, *adjs, *feats, name="gather")


def middle_kernel(
    start, messages, own, adj_x, adj_z, xb, zb, norm, w_neigh, cotangent,
    out, pre_grad, grad, out_buffer, sem,
):
    kind = out.dtype
    inverse = 1.0 / norm[...]
    total = messages[...] + dot(adj_x[:, start:], xb[...]) + dot(adj_z[:, start:], zb[...])
    aggregate = (total * inverse).astype(kind)
    v = own[...] + dot(aggregate, w_neigh[...])
    q = 1.0 / (1.0 + jnp.exp(-v))
    out_buffer[...] = (v * q).astype(kind)
    store = pltpu.make_async_copy(out_buffer, out, sem)
    store.start()
    p = (cotangent[...].astype(jnp.float32) * (q * (1.0 + v * (1.0 - q)))).astype(kind)
    pre_grad[...] = p
    grad[...] = (dot_t(p, w_neigh[...]) * inverse).astype(kind)
    store.wait()


def first_kernel(mine, g, tx, tz):
    rows = tz.shape[0]
    tx[...] = dot(mine[:rows, :], g[...])
    tz[...] = dot(mine[rows:2 * rows, :], g[...])


def second_kernel(theirs, g_sib, tx, tz, xa, xb, za, zb):
    cut, rows = za.shape[0], tz.shape[0]
    z = (tz[...] + dot(theirs[rows:2 * rows, :], g_sib[...])).astype(za.dtype)
    za[...] = z[:cut]
    zb[...] = z[cut:]
    x = tx[...] + dot(theirs[:rows, :], g_sib[...])
    xa[...] = x[:cut]
    xb[...] = x[cut:].astype(xb.dtype)


def add_kernel(a, b, out):
    out[...] = (a[...] + b[...].astype(jnp.float32)).astype(out.dtype)


def own_kernel(mine, theirs, g, g_sib, pre_grad, w_self, out):
    rows = out.shape[0]
    out[...] = (
        dot_t(pre_grad[...], w_self[...])
        + dot(mine[2 * rows:, :], g[...])
        + dot(theirs[2 * rows:, :], g_sib[...])
    )


def last_kernel(own, xa, xb, zb, out, buffer, sem):
    cut = xa.shape[0]
    high = own[cut:, :] + xb[...].astype(jnp.float32) + zb[...].astype(jnp.float32)
    buffer[cut:, :] = high.astype(out.dtype)
    upper = pltpu.make_async_copy(buffer.at[cut:], out.at[cut:], sem.at[0])
    upper.start()
    buffer[:cut, :] = (own[:cut, :] + xa[...].astype(jnp.float32)).astype(out.dtype)
    lower = pltpu.make_async_copy(buffer.at[:cut], out.at[:cut], sem.at[1])
    lower.start()
    upper.wait()
    lower.wait()


def after(value, *earlier):
    return lax.optimization_barrier((value, *earlier))[0]


def per_device(x, w_self, w_neigh, tiles, source_block, edge_counts, normalizer, cotangent):
    n_slab = lax.axis_size("slab")
    ring = range(n_slab)
    pair = [(i, i ^ 1) for i in ring]
    diag = [(i, (i + (1 if i % 2 else -1)) % n_slab) for i in ring]
    hop = [(i, (i + (-2 if i % 2 else 2)) % n_slab) for i in ring]
    back = [(b, a) for a, b in hop]
    swap = [(0, 1), (1, 0)]

    def slab(v, route):
        return lax.ppermute(v, "slab", route)

    def sub(v):
        return lax.ppermute(v, "sub", swap)

    rows, width = x.shape
    cut = rows // 2
    kind = x.dtype
    tiles = pltpu.with_memory_space_constraint(tiles, pltpu.HBM)
    odd = lax.bitwise_and(lax.axis_index("slab"), 1)
    norm = normalizer.astype(jnp.float32)[:, None]
    info = jnp.stack([odd, lax.axis_index("sub")]).astype(jnp.int32)
    sources = source_block.transpose(1, 0, 2)
    counts = edge_counts.transpose(1, 0, 2)
    wide = jax.ShapeDtypeStruct((rows, width), jnp.float32)
    narrow = jax.ShapeDtypeStruct((rows, width), kind)
    half = jax.ShapeDtypeStruct((cut, width), kind)
    half_wide = jax.ShapeDtypeStruct((cut, width), jnp.float32)

    xa = slab(x[:cut], pair)
    x_sib = sub(x)
    high = x[cut:]
    xb = slab(high, pair)
    (fx,) = dense(("pair",), (), False, after(info, high, norm, x_sib), sources, counts, tiles)
    zb = slab(after(high, fx), diag)
    xa = after(xa, fx)
    za = slab(xa, hop)
    xa_sib = sub(xa)
    fz, fo, mine, send = dense(
        ("across", "own"), (fx,), True, after(info, xa), sources, counts, tiles
    )
    theirs = sub(send)
    messages = call(local_kernel, wide, fo, x, x_sib, name="local")
    za = after(za, messages)
    za_sib = sub(za)
    messages = gather(messages, (0, rows), (fx, fx), (xa, xa_sib))
    xb, zb, theirs = lax.optimization_barrier((xb, zb, theirs, messages))[:3]
    xb_sib, zb_sib = sub(xb), sub(zb)
    messages = gather(messages, (0, rows, cut, cut), (fz, fz, fx, fz), (za, za_sib, xb, zb))
    own = call(self_kernel, wide, after(x, messages), w_self, name="self")
    node_out, pre_grad, g = call(
        functools.partial(middle_kernel, rows + cut),
        [narrow, narrow, narrow],
        messages, own, fx, fz, xb_sib, zb_sib, norm, w_neigh, cotangent,
        out_specs=[ANY, VMEM, VMEM],
        scratch=[pltpu.VMEM((rows, width), kind), pltpu.SemaphoreType.DMA],
        name="middle",
    )
    g_sib = sub(g)

    tx, tz = call(first_kernel, [wide, wide], mine, g, name="first")
    pxa, pxb, pza, pzb = call(
        second_kernel, [half_wide, half, half, half], theirs, g_sib, tx, tz, name="second"
    )
    ra = slab(pza, back)
    rxb = slab(pxb, pair)
    own_grad = call(own_kernel, wide, mine, theirs, g, g_sib, after(pre_grad, pxb), w_self, name="own")
    rzb = slab(after(pzb, own_grad), diag)
    rxa = slab(call(add_kernel, half, pxa, after(ra, own_grad), name="add"), pair)
    node_grad = call(
        last_kernel, narrow, own_grad, rxa, rxb, rzb,
        out_specs=ANY,
        scratch=[pltpu.VMEM((rows, width), kind), pltpu.SemaphoreType.DMA((2,))],
        name="last",
    )
    return (node_out, node_grad)


def solution(mesh):
    whole = P(None, None)
    return jax.shard_map(
        per_device,
        mesh=mesh,
        in_specs=(
            P(ROWS, None),
            whole,
            whole,
            P(ROWS, None, None, None, None),
            P(ROWS, None, None),
            P(ROWS, None, None),
            P(ROWS),
            P(ROWS, None),
        ),
        out_specs=(P(ROWS, None), P(ROWS, None)),
        check_vma=False,
    )
```

```python
import functools

import jax
import jax.numpy as jnp
from jax import lax
from jax.experimental import pallas as pl
from jax.experimental.pallas import tpu as pltpu
from jax.sharding import PartitionSpec as P

ROWS = ("parts", "slab", "sub")
VMEM = pl.BlockSpec(memory_space=pltpu.VMEM)
ANY = pl.BlockSpec(memory_space=pl.ANY)


def dot(a, b):
    return jnp.dot(a, b, preferred_element_type=jnp.float32)


def dot_t(a, b):
    return lax.dot_general(a, b, (((1,), (1,)), ((), ())), preferred_element_type=jnp.float32)


def call(kernel, outs, *args, specs=None, out_specs=None, scratch=(), flops=1 << 34, name=None):
    single = not isinstance(outs, list)
    return pl.pallas_call(
        kernel,
        in_specs=specs or [VMEM] * len(args),
        out_specs=out_specs or (VMEM if single else [VMEM] * len(outs)),
        out_shape=outs,
        scratch_shapes=scratch,
        compiler_params=pltpu.CompilerParams(vmem_limit_bytes=12 << 20),
        cost_estimate=pl.CostEstimate(flops=flops, bytes_accessed=flops >> 8, transcendentals=0),
        name=name,
    )(*args)


OFFSET = {
    "own": lambda odd: 1,
    "pair": lambda odd: 2 - 2 * odd,
    "across": lambda odd: 2 * odd,
}


def dense_kernel(roles, known, sources_hbm, counts_hbm, tiles, *refs):
    count = len(roles)
    fwds, refs = refs[:known], refs[known:]
    outs, refs = refs[:count], refs[count:]
    last = len(refs) > 6
    if last:
        mine, send, buffer, total, in_sem, sources, counts, index_sem, turned, out_sem = refs
    else:
        buffer, total, in_sem, sources, counts, index_sem = refs
    local, slots, size = buffer.shape[1], buffer.shape[2], buffer.shape[3]
    rows = local * size
    u = lax.axis_index("sub")
    odd = lax.bitwise_and(lax.axis_index("slab"), 1)
    offsets = [OFFSET[role](odd) for role in roles]
    indices = [
        pltpu.make_async_copy(source, target, index_sem.at[n])
        for n, (source, target) in enumerate(((sources_hbm, sources), (counts_hbm, counts)))
    ]
    for copy in indices:
        copy.start()

    def load(r, i):
        return pltpu.make_async_copy(tiles.at[i, offsets[r]], buffer.at[r, i], in_sem.at[r, i])

    def place_of(b):
        at = (b % local) * size
        return b // local, slice(at, at + size)

    stores = []

    def hand_out(n):
        for h, out in enumerate((mine, send)):
            part = pl.ds(n * rows, rows)
            store = pltpu.make_async_copy(turned.at[h, part], out.at[part], out_sem.at[h, n])
            store.start()
            stores.append(store)

    for r in range(count):
        for i in range(local):
            load(r, i).start()
    if last:
        for n, fwd in enumerate(fwds):
            for i in range(local):
                rows_i = slice(i * size, (i + 1) * size)
                for b in range(2 * local):
                    h, at = place_of(b)
                    block = fwd[rows_i, b * size:(b + 1) * size]
                    turned[h, n * rows + at.start:n * rows + at.stop, rows_i] = block.T
            hand_out(n)
    for copy in indices:
        copy.wait()
    for r in range(count):
        n = known + r
        for i in range(local):
            load(r, i).wait()
            total[...] = jnp.zeros_like(total)
            for k in range(slots):
                b = sources[offsets[r], i, k]
                place = jnp.bitwise_xor(b // local, u) * local + b % local
                scale = counts[offsets[r], i, k].astype(jnp.float32) * (1.0 / size)
                total[place] += buffer[r, i, k].astype(jnp.float32) * scale
            rows_i = slice(i * size, (i + 1) * size)
            for b in range(2 * local):
                block = total[b].astype(outs[r].dtype)
                outs[r][rows_i, b * size:(b + 1) * size] = block
                if last:
                    h, at = place_of(b)
                    turned[h, n * rows + at.start:n * rows + at.stop, rows_i] = block.T
        if last:
            hand_out(n)
    for store in stores:
        store.wait()


def dense(roles, built, last, sources, counts, tiles):
    local, _, slots, size, _ = tiles.shape
    rows = local * size
    count, every = len(roles), len(roles) + len(built)
    kind = tiles.dtype
    hbm = pl.BlockSpec(memory_space=pltpu.HBM)
    outs = [jax.ShapeDtypeStruct((rows, 2 * rows), kind)] * count
    out_specs = [VMEM] * count
    scratch = [
        pltpu.VMEM((count, local, slots, size, size), kind),
        pltpu.VMEM((2 * local, size, size), jnp.float32),
        pltpu.SemaphoreType.DMA((count, local)),
        pltpu.SMEM(sources.shape, jnp.int32),
        pltpu.SMEM(counts.shape, jnp.int32),
        pltpu.SemaphoreType.DMA((2,)),
    ]
    if last:
        outs += [pltpu.HBM((every * rows, rows), kind)] * 2
        out_specs += [hbm] * 2
        scratch += [
            pltpu.VMEM((2, every * rows, rows), kind),
            pltpu.SemaphoreType.DMA((2, every)),
        ]
    sources, counts = (pltpu.with_memory_space_constraint(v, pltpu.HBM) for v in (sources, counts))
    return call(
        functools.partial(dense_kernel, roles, len(built)),
        outs,
        sources, counts, tiles, *built,
        specs=[hbm] * 3 + [VMEM] * len(built),
        out_specs=out_specs,
        scratch=scratch,
        flops=count << 26,
        name="dense_" + roles[0],
    )


def split_kernel(x, low, high, sems):
    cut = low.shape[0]
    parts = [
        pltpu.make_async_copy(x.at[:cut], low, sems.at[0]),
        pltpu.make_async_copy(x.at[cut:], high, sems.at[1]),
    ]
    for part in parts:
        part.start()
    for part in parts:
        part.wait()


def local_kernel(adj, x, x_sib, w_self, messages, own):
    rows = x.shape[0]
    messages[...] = dot(adj[:, :rows], x[...]) + dot(adj[:, rows:], x_sib[...])
    own[...] = dot(x[...], w_self[...])


def gather_kernel(starts, messages, *refs):
    count = len(starts)
    adjs, feats, out = refs[:count], refs[count:2 * count], refs[2 * count]
    total = messages[...]
    for start, adj, feat in zip(starts, adjs, feats):
        total += dot(adj[:, start:start + feat.shape[0]], feat[...])
    out[...] = total


def gather(messages, starts, adjs, feats):
    out = jax.ShapeDtypeStruct(messages.shape, jnp.float32)
    return call(functools.partial(gather_kernel, starts), out, messages, *adjs, *feats, name="gather")


def middle_kernel(
    start, messages, own, adj, last, norm, w_neigh, cotangent,
    out, pre_grad, grad, out_buffer, sem,
):
    kind = out.dtype
    across = (1.0 / norm[...].astype(jnp.float32)).T
    inverse = jnp.concatenate([across[:, b:b + 1] for b in range(across.shape[1])], axis=0)
    total = messages[...] + dot(adj[:, start:], last[...])
    aggregate = (total * inverse).astype(kind)
    v = own[...] + dot(aggregate, w_neigh[...])
    q = 1.0 / (1.0 + jnp.exp(-v))
    out_buffer[...] = (v * q).astype(kind)
    store = pltpu.make_async_copy(out_buffer, out, sem)
    store.start()
    p = (cotangent[...].astype(jnp.float32) * (q * (1.0 + v * (1.0 - q)))).astype(kind)
    pre_grad[...] = p
    grad[...] = (dot_t(p, w_neigh[...]) * inverse).astype(kind)
    store.wait()


def first_kernel(mine, g, theirs, tx, tz, kept, sem):
    rows = tz.shape[0]
    fetch = pltpu.make_async_copy(theirs.at[:2 * rows], kept, sem)
    fetch.start()
    tx[...] = dot(mine[:rows, :], g[...])
    tz[...] = dot(mine[rows:2 * rows, :], g[...])
    fetch.wait()


def second_kernel(theirs, g_sib, tx, tz, px, *pz):
    rows, step = tz.shape[0], pz[0].shape[0]
    z = (tz[...] + dot(theirs[rows:2 * rows, :], g_sib[...])).astype(pz[0].dtype)
    for n, part in enumerate(pz):
        part[...] = z[n * step:(n + 1) * step]
    px[...] = tx[...] + dot(theirs[:rows, :], g_sib[...])


def add_kernel(start, px, b, out):
    part = px[start:start + b.shape[0], :]
    out[...] = (part + b[...].astype(jnp.float32)).astype(out.dtype)


def own_kernel(mine, theirs, g, g_sib, pre_grad, w_self, out):
    rows = out.shape[0]
    out[...] = (
        dot_t(pre_grad[...], w_self[...])
        + dot(mine[2 * rows:, :], g[...])
        + dot(theirs[2 * rows:, :], g_sib[...])
    )


def last_kernel(own, *refs):
    parts, (out, buffer, sem) = refs[:-3], refs[-3:]
    step = parts[0].shape[0]
    stores = []
    for n, part in enumerate(parts):
        at = pl.ds(n * step, step)
        buffer[at, :] = (own[at, :] + part[...].astype(jnp.float32)).astype(out.dtype)
        store = pltpu.make_async_copy(buffer.at[at], out.at[at], sem.at[n])
        store.start()
        stores.append(store)
    for store in stores:
        store.wait()


def after(value, *earlier):
    return lax.optimization_barrier((value, *earlier))[0]


def per_device(x, w_self, w_neigh, tiles, source_block, edge_counts, normalizer, cotangent):
    n_slab = lax.axis_size("slab")
    ring = range(n_slab)
    pair = [(i, i ^ 1) for i in ring]
    hop = [(i, (i + (-2 if i % 2 else 2)) % n_slab) for i in ring]
    back = [(b, a) for a, b in hop]
    swap = [(0, 1), (1, 0)]

    def slab(v, route):
        return lax.ppermute(v, "slab", route)

    def sub(v):
        return lax.ppermute(v, "sub", swap)

    rows, width = x.shape
    cut = rows // 2
    kind = x.dtype
    tiles = pltpu.with_memory_space_constraint(tiles, pltpu.HBM)
    block = tiles.shape[-1]
    norm = normalizer.reshape(rows // block, block)
    sources = source_block.transpose(1, 0, 2)
    counts = edge_counts.transpose(1, 0, 2)
    wide = jax.ShapeDtypeStruct((rows, width), jnp.float32)
    narrow = jax.ShapeDtypeStruct((rows, width), kind)
    half = jax.ShapeDtypeStruct((cut, width), kind)

    low, high = call(
        split_kernel, [half, half], pltpu.with_memory_space_constraint(x, pltpu.HBM),
        specs=[pl.BlockSpec(memory_space=pltpu.HBM)],
        scratch=[pltpu.SemaphoreType.DMA((2,))],
        name="split",
    )
    xa = slab(low, pair)
    x_sib = sub(x)
    (fx,) = dense(("pair",), (), False, after(sources, low, x_sib), counts, tiles)
    xb = slab(high, pair)
    fz, fo, mine, send = dense(("across", "own"), (fx,), True, after(sources, fx), counts, tiles)
    xa = after(xa, fz)
    za = slab(xa, hop)
    xa_sib = sub(xa)
    theirs = sub(send)
    messages, own = call(local_kernel, [wide, wide], fo, x, x_sib, w_self, name="local")
    xb = after(xb, messages)
    zb = slab(xb, hop)
    xb_sib = sub(xb)
    messages = gather(messages, (0, rows, cut), (fx, fx, fx), (xa, xa_sib, xb))
    za, theirs = lax.optimization_barrier((za, theirs, messages))[:2]
    za_sib = sub(za)
    messages = gather(messages, (rows + cut, 0), (fx, fz), (xb_sib, za))
    zb = after(zb, messages)
    zb_sib = sub(zb)
    messages = gather(messages, (rows, cut), (fz, fz), (za_sib, zb))
    node_out, pre_grad, g = call(
        functools.partial(middle_kernel, rows + cut),
        [narrow, narrow, narrow],
        messages, own, fz, zb_sib, norm, w_neigh, cotangent,
        out_specs=[ANY, VMEM, VMEM],
        scratch=[pltpu.VMEM((rows, width), kind), pltpu.SemaphoreType.DMA],
        name="middle",
    )
    g_sib = sub(g)

    tx, tz, theirs_near = call(
        first_kernel, [wide, wide, jax.ShapeDtypeStruct((2 * rows, width), kind)],
        mine, g, theirs,
        specs=[VMEM, VMEM, pl.BlockSpec(memory_space=pltpu.HBM)],
        scratch=[pltpu.SemaphoreType.DMA],
        name="first",
    )
    steps = range(0, rows, block)
    part = jax.ShapeDtypeStruct((block, width), kind)
    px, *pz = call(
        second_kernel, [wide] + [part for _ in steps], theirs_near, g_sib, tx, tz, name="second"
    )
    relayed = [slab(v, back) for v in pz]
    own_grad = call(own_kernel, wide, mine, theirs, g, g_sib, after(pre_grad, px), w_self, name="own")
    summed = []
    for at, v in zip(steps, relayed):
        v = call(functools.partial(add_kernel, at), part, px, after(v, own_grad), name="add")
        summed.append(slab(v, pair))
    node_grad = call(
        last_kernel, narrow, own_grad, *summed,
        out_specs=ANY,
        scratch=[pltpu.VMEM((rows, width), kind), pltpu.SemaphoreType.DMA((len(steps),))],
        name="last",
    )
    return (node_out, node_grad)


def solution(mesh):
    whole = P(None, None)
    return jax.shard_map(
        per_device,
        mesh=mesh,
        in_specs=(
            P(ROWS, None),
            whole,
            whole,
            P(ROWS, None, None, None, None),
            P(ROWS, None, None),
            P(ROWS, None, None),
            P(ROWS),
            P(ROWS, None),
        ),
        out_specs=(P(ROWS, None), P(ROWS, None)),
        check_vma=False,
    )
```

```python
import functools

import jax
import jax.numpy as jnp
from jax import lax
from jax.experimental import pallas as pl
from jax.experimental.pallas import tpu as pltpu
from jax.sharding import PartitionSpec as P

ROWS = ("parts", "slab", "sub")
VMEM = pl.BlockSpec(memory_space=pltpu.VMEM)
ANY = pl.BlockSpec(memory_space=pl.ANY)


def dot(a, b):
    return jnp.dot(a, b, preferred_element_type=jnp.float32)


def dot_t(a, b):
    return lax.dot_general(a, b, (((1,), (1,)), ((), ())), preferred_element_type=jnp.float32)


def call(kernel, outs, *args, specs=None, out_specs=None, scratch=(), flops=1 << 34, name=None):
    single = not isinstance(outs, list)
    return pl.pallas_call(
        kernel,
        in_specs=specs or [VMEM] * len(args),
        out_specs=out_specs or (VMEM if single else [VMEM] * len(outs)),
        out_shape=outs,
        scratch_shapes=scratch,
        compiler_params=pltpu.CompilerParams(vmem_limit_bytes=12 << 20),
        cost_estimate=pl.CostEstimate(flops=flops, bytes_accessed=flops >> 8, transcendentals=0),
        name=name,
    )(*args)


OFFSET = {
    "own": lambda odd: 1,
    "pair": lambda odd: 2 - 2 * odd,
    "across": lambda odd: 2 * odd,
}


def dense_kernel(roles, known, sources_hbm, counts_hbm, tiles, *refs):
    count = len(roles)
    fwds, refs = refs[:known], refs[known:]
    outs, refs = refs[:count], refs[count:]
    last = len(refs) > 6
    if last:
        mine, send, buffer, total, in_sem, sources, counts, index_sem, turned, out_sem = refs
    else:
        buffer, total, in_sem, sources, counts, index_sem = refs
    local, slots, size = buffer.shape[1], buffer.shape[2], buffer.shape[3]
    rows = local * size
    u = lax.axis_index("sub")
    odd = lax.bitwise_and(lax.axis_index("slab"), 1)
    offsets = [OFFSET[role](odd) for role in roles]
    indices = [
        pltpu.make_async_copy(source, target, index_sem.at[n])
        for n, (source, target) in enumerate(((sources_hbm, sources), (counts_hbm, counts)))
    ]
    for copy in indices:
        copy.start()

    def load(r, i):
        return pltpu.make_async_copy(tiles.at[i, offsets[r]], buffer.at[r, i], in_sem.at[r, i])

    def place_of(b):
        at = (b % local) * size
        return b // local, slice(at, at + size)

    stores = []

    def hand_out(n):
        for h, out in enumerate((mine, send)):
            part = pl.ds(n * rows, rows)
            store = pltpu.make_async_copy(turned.at[h, part], out.at[part], out_sem.at[h, n])
            store.start()
            stores.append(store)

    for r in range(count):
        for i in range(local):
            load(r, i).start()
    if last:
        for n, fwd in enumerate(fwds):
            for i in range(local):
                rows_i = slice(i * size, (i + 1) * size)
                for b in range(2 * local):
                    h, at = place_of(b)
                    block = fwd[rows_i, b * size:(b + 1) * size]
                    turned[h, n * rows + at.start:n * rows + at.stop, rows_i] = block.T
            hand_out(n)
    for copy in indices:
        copy.wait()
    for r in range(count):
        n = known + r
        for i in range(local):
            load(r, i).wait()
            total[...] = jnp.zeros_like(total)
            for k in range(slots):
                b = sources[offsets[r], i, k]
                place = jnp.bitwise_xor(b // local, u) * local + b % local
                scale = counts[offsets[r], i, k].astype(jnp.float32) * (1.0 / size)
                total[place] += buffer[r, i, k].astype(jnp.float32) * scale
            rows_i = slice(i * size, (i + 1) * size)
            for b in range(2 * local):
                block = total[b].astype(outs[r].dtype)
                outs[r][rows_i, b * size:(b + 1) * size] = block
                if last:
                    h, at = place_of(b)
                    turned[h, n * rows + at.start:n * rows + at.stop, rows_i] = block.T
        if last:
            hand_out(n)
    for store in stores:
        store.wait()


def dense(roles, built, last, sources, counts, tiles):
    local, _, slots, size, _ = tiles.shape
    rows = local * size
    count, every = len(roles), len(roles) + len(built)
    kind = tiles.dtype
    hbm = pl.BlockSpec(memory_space=pltpu.HBM)
    outs = [jax.ShapeDtypeStruct((rows, 2 * rows), kind)] * count
    out_specs = [VMEM] * count
    scratch = [
        pltpu.VMEM((count, local, slots, size, size), kind),
        pltpu.VMEM((2 * local, size, size), jnp.float32),
        pltpu.SemaphoreType.DMA((count, local)),
        pltpu.SMEM(sources.shape, jnp.int32),
        pltpu.SMEM(counts.shape, jnp.int32),
        pltpu.SemaphoreType.DMA((2,)),
    ]
    if last:
        outs += [pltpu.HBM((every * rows, rows), kind)] * 2
        out_specs += [hbm] * 2
        scratch += [
            pltpu.VMEM((2, every * rows, rows), kind),
            pltpu.SemaphoreType.DMA((2, every)),
        ]
    sources, counts = (pltpu.with_memory_space_constraint(v, pltpu.HBM) for v in (sources, counts))
    return call(
        functools.partial(dense_kernel, roles, len(built)),
        outs,
        sources, counts, tiles, *built,
        specs=[hbm] * 3 + [VMEM] * len(built),
        out_specs=out_specs,
        scratch=scratch,
        flops=count << 26,
        name="dense_" + roles[0],
    )


def split_kernel(x, low, high, sems):
    cut = low.shape[0]
    parts = [
        pltpu.make_async_copy(x.at[:cut], low, sems.at[0]),
        pltpu.make_async_copy(x.at[cut:], high, sems.at[1]),
    ]
    for part in parts:
        part.start()
    for part in parts:
        part.wait()


def local_kernel(adj, x, x_sib, w_self, messages, own):
    rows = x.shape[0]
    messages[...] = dot(adj[:, :rows], x[...]) + dot(adj[:, rows:], x_sib[...])
    own[...] = dot(x[...], w_self[...])


def gather_kernel(starts, messages, *refs):
    count = len(starts)
    adjs, feats, out = refs[:count], refs[count:2 * count], refs[2 * count]
    total = messages[...]
    for start, adj, feat in zip(starts, adjs, feats):
        total += dot(adj[:, start:start + feat.shape[0]], feat[...])
    out[...] = total


def gather(messages, starts, adjs, feats):
    out = jax.ShapeDtypeStruct(messages.shape, jnp.float32)
    return call(functools.partial(gather_kernel, starts), out, messages, *adjs, *feats, name="gather")


def middle_kernel(
    start, messages, own, adj, last, norm, w_neigh, cotangent,
    out, pre_grad, grad, out_buffer, sem,
):
    kind = out.dtype
    across = (1.0 / norm[...].astype(jnp.float32)).T
    inverse = jnp.concatenate([across[:, b:b + 1] for b in range(across.shape[1])], axis=0)
    total = messages[...] + dot(adj[:, start:], last[...])
    aggregate = (total * inverse).astype(kind)
    v = own[...] + dot(aggregate, w_neigh[...])
    q = 1.0 / (1.0 + jnp.exp(-v))
    out_buffer[...] = (v * q).astype(kind)
    store = pltpu.make_async_copy(out_buffer, out, sem)
    store.start()
    p = (cotangent[...].astype(jnp.float32) * (q * (1.0 + v * (1.0 - q)))).astype(kind)
    pre_grad[...] = p
    grad[...] = (dot_t(p, w_neigh[...]) * inverse).astype(kind)
    store.wait()


def first_kernel(mine, g, theirs, tx, tz, kept, sem):
    rows = tz.shape[0]
    fetch = pltpu.make_async_copy(theirs.at[:2 * rows], kept, sem)
    fetch.start()
    tx[...] = dot(mine[:rows, :], g[...])
    tz[...] = dot(mine[rows:2 * rows, :], g[...])
    fetch.wait()


def across_kernel(theirs, g_sib, tz, *pz):
    rows = tz.shape[0]
    z = (tz[...] + dot(theirs[rows:, :], g_sib[...])).astype(pz[0].dtype)
    at = 0
    for part in pz:
        part[...] = z[at:at + part.shape[0]]
        at += part.shape[0]


def add_kernel(start, px, b, out):
    part = px[start:start + b.shape[0], :]
    out[...] = (part + b[...].astype(jnp.float32)).astype(out.dtype)


def own_kernel(mine, theirs, near, g, g_sib, tx, pre_grad, w_self, px, out):
    rows = out.shape[0]
    px[...] = tx[...] + dot(near[:rows, :], g_sib[...])
    out[...] = (
        dot_t(pre_grad[...], w_self[...])
        + dot(mine[2 * rows:, :], g[...])
        + dot(theirs[2 * rows:, :], g_sib[...])
    )


def last_kernel(own, *refs):
    parts, (out, buffer, sem) = refs[:-3], refs[-3:]
    stores, start = [], 0
    for n, part in enumerate(parts):
        at = pl.ds(start, part.shape[0])
        buffer[at, :] = (own[at, :] + part[...].astype(jnp.float32)).astype(out.dtype)
        store = pltpu.make_async_copy(buffer.at[at], out.at[at], sem.at[n])
        store.start()
        stores.append(store)
        start += part.shape[0]
    for store in stores:
        store.wait()


def after(value, *earlier):
    return lax.optimization_barrier((value, *earlier))[0]


def per_device(x, w_self, w_neigh, tiles, source_block, edge_counts, normalizer, cotangent):
    n_slab = lax.axis_size("slab")
    ring = range(n_slab)
    pair = [(i, i ^ 1) for i in ring]
    hop = [(i, (i + (-2 if i % 2 else 2)) % n_slab) for i in ring]
    back = [(b, a) for a, b in hop]
    swap = [(0, 1), (1, 0)]

    def slab(v, route):
        return lax.ppermute(v, "slab", route)

    def sub(v):
        return lax.ppermute(v, "sub", swap)

    rows, width = x.shape
    cut = rows // 2
    kind = x.dtype
    tiles = pltpu.with_memory_space_constraint(tiles, pltpu.HBM)
    block = tiles.shape[-1]
    norm = normalizer.reshape(rows // block, block)
    sources = source_block.transpose(1, 0, 2)
    counts = edge_counts.transpose(1, 0, 2)
    wide = jax.ShapeDtypeStruct((rows, width), jnp.float32)
    narrow = jax.ShapeDtypeStruct((rows, width), kind)
    half = jax.ShapeDtypeStruct((cut, width), kind)

    low, high = call(
        split_kernel, [half, half], pltpu.with_memory_space_constraint(x, pltpu.HBM),
        specs=[pl.BlockSpec(memory_space=pltpu.HBM)],
        scratch=[pltpu.SemaphoreType.DMA((2,))],
        name="split",
    )
    xa = slab(low, pair)
    x_sib = sub(x)
    (fx,) = dense(("pair",), (), False, after(sources, low, x_sib), counts, tiles)
    xb = slab(high, pair)
    fz, fo, mine, send = dense(("across", "own"), (fx,), True, after(sources, fx), counts, tiles)
    xa = after(xa, fz)
    za = slab(xa, hop)
    xa_sib = sub(xa)
    theirs = sub(send)
    messages, own = call(local_kernel, [wide, wide], fo, x, x_sib, w_self, name="local")
    xb = after(xb, messages)
    zb = slab(xb, hop)
    xb_sib = sub(xb)
    messages = gather(messages, (0, rows, cut), (fx, fx, fx), (xa, xa_sib, xb))
    za, theirs = lax.optimization_barrier((za, theirs, messages))[:2]
    za_sib = sub(za)
    messages = gather(messages, (rows + cut, 0), (fx, fz), (xb_sib, za))
    zb = after(zb, messages)
    zb_sib = sub(zb)
    messages = gather(messages, (rows, cut), (fz, fz), (za_sib, zb))
    node_out, pre_grad, g = call(
        functools.partial(middle_kernel, rows + cut),
        [narrow, narrow, narrow],
        messages, own, fz, zb_sib, norm, w_neigh, cotangent,
        out_specs=[ANY, VMEM, VMEM],
        scratch=[pltpu.VMEM((rows, width), kind), pltpu.SemaphoreType.DMA],
        name="middle",
    )
    g_sib = sub(g)

    tx, tz, theirs_near = call(
        first_kernel, [wide, wide, jax.ShapeDtypeStruct((2 * rows, width), kind)],
        mine, g, theirs,
        specs=[VMEM, VMEM, pl.BlockSpec(memory_space=pltpu.HBM)],
        scratch=[pltpu.SemaphoreType.DMA],
        name="first",
    )
    sizes = [block] * (rows // block)
    parts = [jax.ShapeDtypeStruct((n, width), kind) for n in sizes]
    pz = call(across_kernel, parts, theirs_near, g_sib, tz, name="across")
    relayed = [slab(v, back) for v in pz]
    px, own_grad = call(
        own_kernel, [wide, wide],
        mine, theirs, theirs_near, g, g_sib, tx, after(pre_grad, *pz), w_self, name="own",
    )
    summed, at = [], 0
    for part, v in zip(parts, relayed):
        v = call(functools.partial(add_kernel, at), part, px, after(v, own_grad), name="add")
        summed.append(slab(v, pair))
        at += part.shape[0]
    node_grad = call(
        last_kernel, narrow, own_grad, *summed,
        out_specs=ANY,
        scratch=[pltpu.VMEM((rows, width), kind), pltpu.SemaphoreType.DMA((len(parts),))],
        name="last",
    )
    return (node_out, node_grad)


def solution(mesh):
    whole = P(None, None)
    return jax.shard_map(
        per_device,
        mesh=mesh,
        in_specs=(
            P(ROWS, None),
            whole,
            whole,
            P(ROWS, None, None, None, None),
            P(ROWS, None, None),
            P(ROWS, None, None),
            P(ROWS),
            P(ROWS, None),
        ),
        out_specs=(P(ROWS, None), P(ROWS, None)),
        check_vma=False,
    )
```

```python
import functools

import jax
import jax.numpy as jnp
from jax import lax
from jax.experimental import pallas as pl
from jax.experimental.pallas import tpu as pltpu
from jax.sharding import PartitionSpec as P

ROWS = ("parts", "slab", "sub")
VMEM = pl.BlockSpec(memory_space=pltpu.VMEM)
ANY = pl.BlockSpec(memory_space=pl.ANY)


def dot(a, b):
    return jnp.dot(a, b, preferred_element_type=jnp.float32)


def dot_t(a, b):
    return lax.dot_general(a, b, (((1,), (1,)), ((), ())), preferred_element_type=jnp.float32)


def call(kernel, outs, *args, specs=None, out_specs=None, scratch=(), flops=1 << 34, name=None):
    single = not isinstance(outs, list)
    return pl.pallas_call(
        kernel,
        in_specs=specs or [VMEM] * len(args),
        out_specs=out_specs or (VMEM if single else [VMEM] * len(outs)),
        out_shape=outs,
        scratch_shapes=scratch,
        compiler_params=pltpu.CompilerParams(vmem_limit_bytes=12 << 20),
        cost_estimate=pl.CostEstimate(flops=flops, bytes_accessed=flops >> 8, transcendentals=0),
        name=name,
    )(*args)


OFFSET = {
    "own": lambda odd: 1,
    "pair": lambda odd: 2 - 2 * odd,
    "across": lambda odd: 2 * odd,
}


def dense_kernel(roles, known, sources_hbm, counts_hbm, tiles, *refs):
    count = len(roles)
    fwds, refs = refs[:known], refs[known:]
    outs, refs = refs[:count], refs[count:]
    last = len(refs) > 6
    if last:
        mine, send, buffer, total, in_sem, sources, counts, index_sem, turned, out_sem = refs
    else:
        buffer, total, in_sem, sources, counts, index_sem = refs
    local, slots, size = buffer.shape[1], buffer.shape[2], buffer.shape[3]
    rows = local * size
    u = lax.axis_index("sub")
    odd = lax.bitwise_and(lax.axis_index("slab"), 1)
    offsets = [OFFSET[role](odd) for role in roles]
    indices = [
        pltpu.make_async_copy(source, target, index_sem.at[n])
        for n, (source, target) in enumerate(((sources_hbm, sources), (counts_hbm, counts)))
    ]
    for copy in indices:
        copy.start()

    def load(r, i):
        return pltpu.make_async_copy(tiles.at[i, offsets[r]], buffer.at[r, i], in_sem.at[r, i])

    def place_of(b):
        at = (b % local) * size
        return b // local, slice(at, at + size)

    stores = []

    def hand_out(n):
        for h, out in enumerate((mine, send)):
            part = pl.ds(n * rows, rows)
            store = pltpu.make_async_copy(turned.at[h, part], out.at[part], out_sem.at[h, n])
            store.start()
            stores.append(store)

    for r in range(count):
        for i in range(local):
            load(r, i).start()
    if last:
        for n, fwd in enumerate(fwds):
            for i in range(local):
                rows_i = slice(i * size, (i + 1) * size)
                for b in range(2 * local):
                    h, at = place_of(b)
                    block = fwd[rows_i, b * size:(b + 1) * size]
                    turned[h, n * rows + at.start:n * rows + at.stop, rows_i] = block.T
            hand_out(n)
    for copy in indices:
        copy.wait()
    for r in range(count):
        n = known + r
        for i in range(local):
            load(r, i).wait()
            total[...] = jnp.zeros_like(total)
            for k in range(slots):
                b = sources[offsets[r], i, k]
                place = jnp.bitwise_xor(b // local, u) * local + b % local
                scale = counts[offsets[r], i, k].astype(jnp.float32) * (1.0 / size)
                total[place] += buffer[r, i, k].astype(jnp.float32) * scale
            rows_i = slice(i * size, (i + 1) * size)
            for b in range(2 * local):
                block = total[b].astype(outs[r].dtype)
                outs[r][rows_i, b * size:(b + 1) * size] = block
                if last:
                    h, at = place_of(b)
                    turned[h, n * rows + at.start:n * rows + at.stop, rows_i] = block.T
        if last:
            hand_out(n)
    for store in stores:
        store.wait()


def dense(roles, built, last, sources, counts, tiles):
    local, _, slots, size, _ = tiles.shape
    rows = local * size
    count, every = len(roles), len(roles) + len(built)
    kind = tiles.dtype
    hbm = pl.BlockSpec(memory_space=pltpu.HBM)
    outs = [jax.ShapeDtypeStruct((rows, 2 * rows), kind)] * count
    out_specs = [VMEM] * count
    scratch = [
        pltpu.VMEM((count, local, slots, size, size), kind),
        pltpu.VMEM((2 * local, size, size), jnp.float32),
        pltpu.SemaphoreType.DMA((count, local)),
        pltpu.SMEM(sources.shape, jnp.int32),
        pltpu.SMEM(counts.shape, jnp.int32),
        pltpu.SemaphoreType.DMA((2,)),
    ]
    if last:
        outs += [pltpu.HBM((every * rows, rows), kind)] * 2
        out_specs += [hbm] * 2
        scratch += [
            pltpu.VMEM((2, every * rows, rows), kind),
            pltpu.SemaphoreType.DMA((2, every)),
        ]
    sources, counts = (pltpu.with_memory_space_constraint(v, pltpu.HBM) for v in (sources, counts))
    return call(
        functools.partial(dense_kernel, roles, len(built)),
        outs,
        sources, counts, tiles, *built,
        specs=[hbm] * 3 + [VMEM] * len(built),
        out_specs=out_specs,
        scratch=scratch,
        flops=count << 26,
        name="dense_" + roles[0],
    )


def split_kernel(x, low, high, sems):
    cut = low.shape[0]
    parts = [
        pltpu.make_async_copy(x.at[:cut], low, sems.at[0]),
        pltpu.make_async_copy(x.at[cut:], high, sems.at[1]),
    ]
    for part in parts:
        part.start()
    for part in parts:
        part.wait()


def local_kernel(adj, x, x_sib, w_self, messages, own):
    rows = x.shape[0]
    messages[...] = dot(adj[:, :rows], x[...]) + dot(adj[:, rows:], x_sib[...])
    own[...] = dot(x[...], w_self[...])


def gather_kernel(starts, messages, *refs):
    count = len(starts)
    adjs, feats, out = refs[:count], refs[count:2 * count], refs[2 * count]
    total = messages[...]
    for start, adj, feat in zip(starts, adjs, feats):
        total += dot(adj[:, start:start + feat.shape[0]], feat[...])
    out[...] = total


def gather(messages, starts, adjs, feats):
    out = jax.ShapeDtypeStruct(messages.shape, jnp.float32)
    return call(functools.partial(gather_kernel, starts), out, messages, *adjs, *feats, name="gather")


def middle_kernel(
    start, messages, own, adj, last, norm, w_neigh, cotangent,
    out, pre_grad, grad,
):
    kind = out.dtype
    across = (1.0 / norm[...].astype(jnp.float32)).T
    inverse = jnp.concatenate([across[:, b:b + 1] for b in range(across.shape[1])], axis=0)
    total = messages[...] + dot(adj[:, start:], last[...])
    aggregate = (total * inverse).astype(kind)
    v = own[...] + dot(aggregate, w_neigh[...])
    q = 1.0 / (1.0 + jnp.exp(-v))
    out[...] = (v * q).astype(kind)
    p = (cotangent[...].astype(jnp.float32) * (q * (1.0 + v * (1.0 - q)))).astype(kind)
    pre_grad[...] = p
    grad[...] = (dot_t(p, w_neigh[...]) * inverse).astype(kind)


def first_kernel(mine, g, theirs, near, tx, tz, kept, out, sems):
    rows = tz.shape[0]
    fetch = pltpu.make_async_copy(theirs.at[:2 * rows], kept, sems.at[0])
    store = pltpu.make_async_copy(near, out, sems.at[1])
    fetch.start()
    store.start()
    tx[...] = dot(mine[:rows, :], g[...])
    tz[...] = dot(mine[rows:2 * rows, :], g[...])
    fetch.wait()
    store.wait()


def across_kernel(theirs, g_sib, tz, *pz):
    rows = tz.shape[0]
    z = (tz[...] + dot(theirs[rows:, :], g_sib[...])).astype(pz[0].dtype)
    at = 0
    for part in pz:
        part[...] = z[at:at + part.shape[0]]
        at += part.shape[0]


def add_kernel(start, px, b, out):
    part = px[start:start + b.shape[0], :]
    out[...] = (part + b[...].astype(jnp.float32)).astype(out.dtype)


def own_kernel(mine, theirs, near, g, g_sib, tx, pre_grad, w_self, px, out):
    rows = out.shape[0]
    px[...] = tx[...] + dot(near[:rows, :], g_sib[...])
    out[...] = (
        dot_t(pre_grad[...], w_self[...])
        + dot(mine[2 * rows:, :], g[...])
        + dot(theirs[2 * rows:, :], g_sib[...])
    )


def last_kernel(own, *refs):
    parts, (out, buffer, sem) = refs[:-3], refs[-3:]
    stores, start = [], 0
    for n, part in enumerate(parts):
        at = pl.ds(start, part.shape[0])
        buffer[at, :] = (own[at, :] + part[...].astype(jnp.float32)).astype(out.dtype)
        store = pltpu.make_async_copy(buffer.at[at], out.at[at], sem.at[n])
        store.start()
        stores.append(store)
        start += part.shape[0]
    for store in stores:
        store.wait()


def after(value, *earlier):
    return lax.optimization_barrier((value, *earlier))[0]


def per_device(x, w_self, w_neigh, tiles, source_block, edge_counts, normalizer, cotangent):
    n_slab = lax.axis_size("slab")
    ring = range(n_slab)
    pair = [(i, i ^ 1) for i in ring]
    hop = [(i, (i + (-2 if i % 2 else 2)) % n_slab) for i in ring]
    back = [(b, a) for a, b in hop]
    swap = [(0, 1), (1, 0)]

    def slab(v, route):
        return lax.ppermute(v, "slab", route)

    def sub(v):
        return lax.ppermute(v, "sub", swap)

    rows, width = x.shape
    cut = rows // 2
    kind = x.dtype
    tiles = pltpu.with_memory_space_constraint(tiles, pltpu.HBM)
    block = tiles.shape[-1]
    norm = normalizer.reshape(rows // block, block)
    sources = source_block.transpose(1, 0, 2)
    counts = edge_counts.transpose(1, 0, 2)
    wide = jax.ShapeDtypeStruct((rows, width), jnp.float32)
    narrow = jax.ShapeDtypeStruct((rows, width), kind)
    half = jax.ShapeDtypeStruct((cut, width), kind)

    low, high = call(
        split_kernel, [half, half], pltpu.with_memory_space_constraint(x, pltpu.HBM),
        specs=[pl.BlockSpec(memory_space=pltpu.HBM)],
        scratch=[pltpu.SemaphoreType.DMA((2,))],
        name="split",
    )
    xa = slab(low, pair)
    x_sib = sub(x)
    (fx,) = dense(("pair",), (), False, after(sources, low, x_sib), counts, tiles)
    xb = slab(high, pair)
    fz, fo, mine, send = dense(("across", "own"), (fx,), True, after(sources, fx), counts, tiles)
    xa = after(xa, fz)
    za = slab(xa, hop)
    xa_sib = sub(xa)
    theirs = sub(send)
    messages, own = call(local_kernel, [wide, wide], fo, x, x_sib, w_self, name="local")
    xb = after(xb, messages)
    zb = slab(xb, hop)
    xb_sib = sub(xb)
    messages = gather(messages, (0, rows, cut), (fx, fx, fx), (xa, xa_sib, xb))
    za, theirs = lax.optimization_barrier((za, theirs, messages))[:2]
    za_sib = sub(za)
    messages = gather(messages, (rows + cut, 0), (fx, fz), (xb_sib, za))
    zb = after(zb, messages)
    zb_sib = sub(zb)
    messages = gather(messages, (rows, cut), (fz, fz), (za_sib, zb))
    node_out, pre_grad, g = call(
        functools.partial(middle_kernel, rows + cut),
        [narrow, narrow, narrow],
        messages, own, fz, zb_sib, norm, w_neigh, cotangent,
        name="middle",
    )
    g_sib = sub(g)

    tx, tz, theirs_near, node_out = call(
        first_kernel,
        [wide, wide, jax.ShapeDtypeStruct((2 * rows, width), kind), narrow],
        mine, g, theirs, node_out,
        specs=[VMEM, VMEM, pl.BlockSpec(memory_space=pltpu.HBM), VMEM],
        out_specs=[VMEM, VMEM, VMEM, ANY],
        scratch=[pltpu.SemaphoreType.DMA((2,))],
        name="first",
    )
    sizes = [block] * (rows // block)
    parts = [jax.ShapeDtypeStruct((n, width), kind) for n in sizes]
    pz = call(across_kernel, parts, theirs_near, g_sib, tz, name="across")
    relayed = [slab(v, back) for v in pz]
    px, own_grad = call(
        own_kernel, [wide, wide],
        mine, theirs, theirs_near, g, g_sib, tx, after(pre_grad, *pz), w_self, name="own",
    )
    summed, at = [], 0
    for part, v in zip(parts, relayed):
        v = call(functools.partial(add_kernel, at), part, px, after(v, own_grad), name="add")
        summed.append(slab(v, pair))
        at += part.shape[0]
    node_grad = call(
        last_kernel, narrow, own_grad, *summed,
        out_specs=ANY,
        scratch=[pltpu.VMEM((rows, width), kind), pltpu.SemaphoreType.DMA((len(parts),))],
        name="last",
    )
    return (node_out, node_grad)


def solution(mesh):
    whole = P(None, None)
    return jax.shard_map(
        per_device,
        mesh=mesh,
        in_specs=(
            P(ROWS, None),
            whole,
            whole,
            P(ROWS, None, None, None, None),
            P(ROWS, None, None),
            P(ROWS, None, None),
            P(ROWS),
            P(ROWS, None),
        ),
        out_specs=(P(ROWS, None), P(ROWS, None)),
        check_vma=False,
    )
```

```python
import functools

import jax
import jax.numpy as jnp
from jax import lax
from jax.experimental import pallas as pl
from jax.experimental.pallas import tpu as pltpu
from jax.sharding import PartitionSpec as P

ROWS = ("parts", "slab", "sub")
VMEM = pl.BlockSpec(memory_space=pltpu.VMEM)
ANY = pl.BlockSpec(memory_space=pl.ANY)


def dot(a, b):
    return jnp.dot(a, b, preferred_element_type=jnp.float32)


def dot_t(a, b):
    return lax.dot_general(a, b, (((1,), (1,)), ((), ())), preferred_element_type=jnp.float32)


def call(kernel, outs, *args, specs=None, out_specs=None, scratch=(), flops=1 << 34, aliases={}, name=None):
    single = not isinstance(outs, list)
    return pl.pallas_call(
        kernel,
        in_specs=specs or [VMEM] * len(args),
        out_specs=out_specs or (VMEM if single else [VMEM] * len(outs)),
        out_shape=outs,
        scratch_shapes=scratch,
        input_output_aliases=aliases,
        compiler_params=pltpu.CompilerParams(vmem_limit_bytes=12 << 20),
        cost_estimate=pl.CostEstimate(flops=flops, bytes_accessed=flops >> 8, transcendentals=0),
        name=name,
    )(*args)


OFFSET = {
    "own": lambda odd: 1,
    "pair": lambda odd: 2 - 2 * odd,
    "across": lambda odd: 2 * odd,
}


def dense_kernel(roles, known, sources_hbm, counts_hbm, tiles, *refs):
    count = len(roles)
    fwds, refs = refs[:known], refs[known:]
    outs, refs = refs[:count], refs[count:]
    last = len(refs) > 6
    if last:
        mine, send, buffer, total, in_sem, sources, counts, index_sem, turned, out_sem = refs
    else:
        buffer, total, in_sem, sources, counts, index_sem = refs
    local, slots, size = buffer.shape[1], buffer.shape[2], buffer.shape[3]
    rows = local * size
    u = lax.axis_index("sub")
    odd = lax.bitwise_and(lax.axis_index("slab"), 1)
    offsets = [OFFSET[role](odd) for role in roles]
    indices = [
        pltpu.make_async_copy(source, target, index_sem.at[n])
        for n, (source, target) in enumerate(((sources_hbm, sources), (counts_hbm, counts)))
    ]
    for copy in indices:
        copy.start()

    def load(r, i):
        return pltpu.make_async_copy(tiles.at[i, offsets[r]], buffer.at[r, i], in_sem.at[r, i])

    def place_of(b):
        at = (b % local) * size
        return b // local, slice(at, at + size)

    stores = []

    def hand_out(n):
        for h, out in enumerate((mine, send)):
            part = pl.ds(n * rows, rows)
            store = pltpu.make_async_copy(turned.at[h, part], out.at[part], out_sem.at[h, n])
            store.start()
            stores.append(store)

    for r in range(count):
        for i in range(local):
            load(r, i).start()
    if last:
        for n, fwd in enumerate(fwds):
            for i in range(local):
                rows_i = slice(i * size, (i + 1) * size)
                for b in range(2 * local):
                    h, at = place_of(b)
                    block = fwd[rows_i, b * size:(b + 1) * size]
                    turned[h, n * rows + at.start:n * rows + at.stop, rows_i] = block.T
            hand_out(n)
    for copy in indices:
        copy.wait()
    for r in range(count):
        n = known + r
        for i in range(local):
            load(r, i).wait()
            total[...] = jnp.zeros_like(total)
            for k in range(slots):
                b = sources[offsets[r], i, k]
                place = jnp.bitwise_xor(b // local, u) * local + b % local
                scale = counts[offsets[r], i, k].astype(jnp.float32) * (1.0 / size)
                total[place] += buffer[r, i, k].astype(jnp.float32) * scale
            rows_i = slice(i * size, (i + 1) * size)
            for b in range(2 * local):
                block = total[b].astype(outs[r].dtype)
                outs[r][rows_i, b * size:(b + 1) * size] = block
                if last:
                    h, at = place_of(b)
                    turned[h, n * rows + at.start:n * rows + at.stop, rows_i] = block.T
        if last:
            hand_out(n)
    for store in stores:
        store.wait()


def dense(roles, built, last, sources, counts, tiles):
    local, _, slots, size, _ = tiles.shape
    rows = local * size
    count, every = len(roles), len(roles) + len(built)
    kind = tiles.dtype
    hbm = pl.BlockSpec(memory_space=pltpu.HBM)
    outs = [jax.ShapeDtypeStruct((rows, 2 * rows), kind)] * count
    out_specs = [VMEM] * count
    scratch = [
        pltpu.VMEM((count, local, slots, size, size), kind),
        pltpu.VMEM((2 * local, size, size), jnp.float32),
        pltpu.SemaphoreType.DMA((count, local)),
        pltpu.SMEM(sources.shape, jnp.int32),
        pltpu.SMEM(counts.shape, jnp.int32),
        pltpu.SemaphoreType.DMA((2,)),
    ]
    if last:
        outs += [pltpu.HBM((every * rows, rows), kind)] * 2
        out_specs += [hbm] * 2
        scratch += [
            pltpu.VMEM((2, every * rows, rows), kind),
            pltpu.SemaphoreType.DMA((2, every)),
        ]
    sources, counts = (pltpu.with_memory_space_constraint(v, pltpu.HBM) for v in (sources, counts))
    return call(
        functools.partial(dense_kernel, roles, len(built)),
        outs,
        sources, counts, tiles, *built,
        specs=[hbm] * 3 + [VMEM] * len(built),
        out_specs=out_specs,
        scratch=scratch,
        flops=count << 26,
        name="dense_" + roles[0],
    )


def split_kernel(x, low, high, sems):
    cut = low.shape[0]
    parts = [
        pltpu.make_async_copy(x.at[:cut], low, sems.at[0]),
        pltpu.make_async_copy(x.at[cut:], high, sems.at[1]),
    ]
    for part in parts:
        part.start()
    for part in parts:
        part.wait()


def local_kernel(adj, x, x_sib, w_self, messages, own):
    rows = x.shape[0]
    messages[...] = dot(adj[:, :rows], x[...]) + dot(adj[:, rows:], x_sib[...])
    own[...] = dot(x[...], w_self[...])


def gather_kernel(starts, messages, *refs):
    count = len(starts)
    adjs, feats, out = refs[:count], refs[count:2 * count], refs[2 * count]
    total = messages[...]
    for start, adj, feat in zip(starts, adjs, feats):
        total += dot(adj[:, start:start + feat.shape[0]], feat[...])
    out[...] = total


def gather(messages, starts, adjs, feats):
    out = jax.ShapeDtypeStruct(messages.shape, jnp.float32)
    return call(functools.partial(gather_kernel, starts), out, messages, *adjs, *feats, name="gather")


def middle_kernel(
    start, messages, own, adj, last, norm, w_neigh, cotangent,
    out, pre_grad, grad,
):
    kind = out.dtype
    across = (1.0 / norm[...].astype(jnp.float32)).T
    inverse = jnp.concatenate([across[:, b:b + 1] for b in range(across.shape[1])], axis=0)
    total = messages[...] + dot(adj[:, start:], last[...])
    aggregate = (total * inverse).astype(kind)
    v = own[...] + dot(aggregate, w_neigh[...])
    q = 1.0 / (1.0 + jnp.exp(-v))
    out[...] = (v * q).astype(kind)
    p = (cotangent[...].astype(jnp.float32) * (q * (1.0 + v * (1.0 - q)))).astype(kind)
    pre_grad[...] = p
    grad[...] = (dot_t(p, w_neigh[...]) * inverse).astype(kind)


def first_kernel(mine, g, theirs, near, tx, tz, kept, out, sems):
    rows = tz.shape[0]
    fetch = pltpu.make_async_copy(theirs.at[:2 * rows], kept, sems.at[0])
    store = pltpu.make_async_copy(near, out, sems.at[1])
    fetch.start()
    store.start()
    tx[...] = dot(mine[:rows, :], g[...])
    tz[...] = dot(mine[rows:2 * rows, :], g[...])
    fetch.wait()
    store.wait()


def across_kernel(theirs, g_sib, tz, *pz):
    rows = tz.shape[0]
    z = (tz[...] + dot(theirs[rows:, :], g_sib[...])).astype(pz[0].dtype)
    at = 0
    for part in pz:
        part[...] = z[at:at + part.shape[0]]
        at += part.shape[0]


def add_kernel(start, px, b, out):
    part = px[start:start + b.shape[0], :]
    out[...] = (part + b[...].astype(jnp.float32)).astype(out.dtype)


def own_kernel(mine, theirs, near, g, g_sib, tx, pre_grad, w_self, px, out):
    rows = out.shape[0]
    px[...] = tx[...] + dot(near[:rows, :], g_sib[...])
    out[...] = (
        dot_t(pre_grad[...], w_self[...])
        + dot(mine[2 * rows:, :], g[...])
        + dot(theirs[2 * rows:, :], g_sib[...])
    )


def last_kernel(start, own, *refs):
    parts, (out, buffer, sem) = refs[:-3], refs[-3:]
    stores = []
    for n, part in enumerate(p for p in parts if p.shape[0] != out.shape[0]):
        at = pl.ds(start, part.shape[0])
        buffer[at, :] = (own[at, :] + part[...].astype(jnp.float32)).astype(out.dtype)
        store = pltpu.make_async_copy(buffer.at[at], out.at[at], sem.at[n])
        store.start()
        stores.append(store)
        start += part.shape[0]
    for store in stores:
        store.wait()


def after(value, *earlier):
    return lax.optimization_barrier((value, *earlier))[0]


def per_device(x, w_self, w_neigh, tiles, source_block, edge_counts, normalizer, cotangent):
    n_slab = lax.axis_size("slab")
    ring = range(n_slab)
    pair = [(i, i ^ 1) for i in ring]
    hop = [(i, (i + (-2 if i % 2 else 2)) % n_slab) for i in ring]
    back = [(b, a) for a, b in hop]
    swap = [(0, 1), (1, 0)]

    def slab(v, route):
        return lax.ppermute(v, "slab", route)

    def sub(v):
        return lax.ppermute(v, "sub", swap)

    rows, width = x.shape
    cut = rows // 2
    kind = x.dtype
    tiles = pltpu.with_memory_space_constraint(tiles, pltpu.HBM)
    block = tiles.shape[-1]
    norm = normalizer.reshape(rows // block, block)
    sources = source_block.transpose(1, 0, 2)
    counts = edge_counts.transpose(1, 0, 2)
    wide = jax.ShapeDtypeStruct((rows, width), jnp.float32)
    narrow = jax.ShapeDtypeStruct((rows, width), kind)
    half = jax.ShapeDtypeStruct((cut, width), kind)

    low, high = call(
        split_kernel, [half, half], pltpu.with_memory_space_constraint(x, pltpu.HBM),
        specs=[pl.BlockSpec(memory_space=pltpu.HBM)],
        scratch=[pltpu.SemaphoreType.DMA((2,))],
        name="split",
    )
    xa = slab(low, pair)
    x_sib = sub(x)
    (fx,) = dense(("pair",), (), False, after(sources, low, x_sib), counts, tiles)
    xb = slab(high, pair)
    fz, fo, mine, send = dense(("across", "own"), (fx,), True, after(sources, fx), counts, tiles)
    xa = after(xa, fz)
    za = slab(xa, hop)
    xa_sib = sub(xa)
    theirs = sub(send)
    messages, own = call(local_kernel, [wide, wide], fo, x, x_sib, w_self, name="local")
    xb = after(xb, messages)
    zb = slab(xb, hop)
    xb_sib = sub(xb)
    messages = gather(messages, (0, rows, cut), (fx, fx, fx), (xa, xa_sib, xb))
    za, theirs = lax.optimization_barrier((za, theirs, messages))[:2]
    za_sib = sub(za)
    messages = gather(messages, (rows + cut, 0), (fx, fz), (xb_sib, za))
    zb = after(zb, messages)
    zb_sib = sub(zb)
    messages = gather(messages, (rows, cut), (fz, fz), (za_sib, zb))
    node_out, pre_grad, g = call(
        functools.partial(middle_kernel, rows + cut),
        [narrow, narrow, narrow],
        messages, own, fz, zb_sib, norm, w_neigh, cotangent,
        name="middle",
    )
    g_sib = sub(g)

    tx, tz, theirs_near, node_out = call(
        first_kernel,
        [wide, wide, jax.ShapeDtypeStruct((2 * rows, width), kind), narrow],
        mine, g, theirs, node_out,
        specs=[VMEM, VMEM, pl.BlockSpec(memory_space=pltpu.HBM), VMEM],
        out_specs=[VMEM, VMEM, VMEM, ANY],
        scratch=[pltpu.SemaphoreType.DMA((2,))],
        name="first",
    )
    sizes = [block] * (rows // block)
    parts = [jax.ShapeDtypeStruct((n, width), kind) for n in sizes]
    pz = call(across_kernel, parts, theirs_near, g_sib, tz, name="across")
    relayed = [slab(v, back) for v in pz]
    px, own_grad = call(
        own_kernel, [wide, wide],
        mine, theirs, theirs_near, g, g_sib, tx, after(pre_grad, *pz), w_self, name="own",
    )
    summed, at = [], 0
    for part, v in zip(parts, relayed):
        v = call(functools.partial(add_kernel, at), part, px, after(v, own_grad), name="add")
        summed.append(slab(v, pair))
        at += part.shape[0]
    scratch = [pltpu.VMEM((rows, width), kind), pltpu.SemaphoreType.DMA((len(parts),))]
    far = pl.BlockSpec(memory_space=pltpu.HBM)
    most = rows - parts[-1].shape[0]
    node_grad = call(
        functools.partial(last_kernel, 0), pltpu.HBM((rows, width), kind),
        own_grad, *summed[:-1],
        out_specs=far, scratch=scratch, name="most",
    )
    node_grad = call(
        functools.partial(last_kernel, most), pltpu.HBM((rows, width), kind),
        own_grad, summed[-1], node_grad,
        specs=[VMEM, VMEM, far], out_specs=far, scratch=scratch,
        aliases={2: 0}, name="last",
    )
    return (node_out, node_grad)


def solution(mesh):
    whole = P(None, None)
    return jax.shard_map(
        per_device,
        mesh=mesh,
        in_specs=(
            P(ROWS, None),
            whole,
            whole,
            P(ROWS, None, None, None, None),
            P(ROWS, None, None),
            P(ROWS, None, None),
            P(ROWS),
            P(ROWS, None),
        ),
        out_specs=(P(ROWS, None), P(ROWS, None)),
        check_vma=False,
    )
```
